32 devices in a mesh: rep: 4 (over z), shard: 8 (over y, x, core).
Axes of the slice: x: 2, y: 2, z: 4, core: 2. Of those that a mesh axis runs over, the one named last changes fastest.
Arguments:
- hidden_in: bfloat16 [8192, 2048], P(('rep', 'shard')), may hold values from -6 to 6
- cotangent: bfloat16 [8192, 2048], P(('rep', 'shard')), may hold values from -6 to 6
- lengths: int32 [32, 4], P(('rep', 'shard')), may hold values from 0 to 256, as said below
- offsets: int32 [32, 4], P(('rep', 'shard')), may hold values from 0 to 256, as said below
- projection_weight: bfloat16 [2048, 4096], P('shard'), may hold values from -0.125 to 0.125
- merge_weight: bfloat16 [2048, 2048], P('shard'), may hold values from -1 to 1
- expand_weight: bfloat16 [2048, 12288], P('shard'), may hold values from -0.125 to 0.125
- down_weight: bfloat16 [6144, 2048], P('shard'), may hold values from -0.078125 to 0.078125
- first_gain: bfloat16 [2048], P('shard'), may hold values from 0.099609375 to 1.8984375
- second_gain: bfloat16 [2048], P('shard'), may hold values from 0.099609375 to 1.8984375
- query_norm_scale: bfloat16 [128], P('shard'), may hold values from 0.099609375 to 1.8984375
- key_gain: bfloat16 [128], P('shard'), may hold values from 0.099609375 to 1.8984375
Outputs:
- output: bfloat16 [8192, 2048], P(('rep', 'shard'))
- input_grad: bfloat16 [8192, 2048], P(('rep', 'shard'))
- heads_grad: float32 [2048, 4096], P('shard')
- merge_grad: float32 [2048, 2048], P('shard')
- expand_grad: float32 [2048, 12288], P('shard')
- down_grad: float32 [6144, 2048], P('shard')
- first_grad: float32 [2048], P('shard')
- second_grad: float32 [2048], P('shard')
- query_grad: float32 [128], P('shard')
- key_grad: float32 [128], P('shard')
The draws below stay inside these ranges and needn't reach their ends.
Inputs may be any that keep to these rules, and one draw needn't show every extreme that they name: `lengths`: row r belongs to device row r over rep+shard (rep the slower). An entry with length l > 0 and offset o holds one sequence in slots o to o + l - 1 of that device's 256 slots, with o + l <= 256; entries of a row never intersect; length 0 marks an empty entry. Some device holds one sequence of 256 tokens. `offsets`: first slot of each entry of lengths.
All inputs are finite; a program needn't handle non-finite values.
Results may differ from the reference program's by a relative error of at most 0.018.
Values may be sent and summed in bfloat16 or wider, within the bound.
No kernel may reach another device: no remote copies, remote signals or barrier semaphores. Data moves between devices by JAX's collectives and lax.ppermute only.
A program may use at most 448 MiB of HBM per device.

```python
import math
import jax
import jax.numpy as jnp
from jax import lax

MODEL_WIDTH = 2048
QUERY_HEADS = 16
KEY_VALUE_HEADS = 8
HEAD_SIZE = 128
FF = 6144
CAP = 256
NSEQ = 4
NDEV = 32
TOKENS = 8192


def sequence_layout(key):
    base = jax.random.fold_in(key, 7)
    key_rows = jax.random.split(base, 5)
    used = jax.random.randint(key_rows[0], (NDEV,), CAP // 2, CAP + 1)
    full_row = jax.random.randint(key_rows[4], (), 0, NDEV)
    rows = jnp.arange(NDEV, dtype=jnp.int32)
    used = jnp.where(rows == full_row, CAP, used)
    present = jax.random.randint(key_rows[1], (NDEV,), 1, NSEQ + 1)
    present = jnp.where(rows == full_row, 1, present)
    raw = jax.random.randint(key_rows[2], (NDEV, NSEQ - 1), 0, 1 << 20)
    cuts = raw % (used[:, None] + 1)
    rank = jnp.arange(NSEQ - 1, dtype=jnp.int32)[None, :]
    cuts = jnp.where(rank < present[:, None] - 1, cuts, used[:, None])
    cuts = jnp.sort(cuts, axis=1)
    bounds = jnp.concatenate([jnp.zeros((NDEV, 1), jnp.int32), cuts, used[:, None]], axis=1)
    seq_lengths = bounds[:, 1:] - bounds[:, :-1]
    spare = jax.random.randint(key_rows[3], (NDEV,), 0, 1 << 20) % (CAP - used + 1)
    seq_offsets = spare[:, None] + bounds[:, :-1]
    return (seq_lengths.astype(jnp.int32), seq_offsets.astype(jnp.int32))


def draw_lengths(key, part):
    return sequence_layout(key)[0]


def draw_offsets(key, part):
    return sequence_layout(key)[1]


def shard_levels(key, dims, cuts, low, largest):
    def one(dim, blocks):
        draws = jax.random.uniform(jax.random.fold_in(jax.random.fold_in(key, 6), dim), (blocks,), jnp.float32, low / len(cuts), largest / len(cuts))
        return jnp.repeat(jnp.exp(draws), dims[dim] // blocks).reshape((-1,) + (1,) * (len(dims) - dim - 1))

    level = one(*cuts[0])
    for cut in cuts[1:]:
        level = level * one(*cut)
    return level


def bell_draw(rng, dims, spread, bound, shards=(), kind=jnp.bfloat16):
    values = spread * jax.random.normal(rng, dims, jnp.float32)
    if shards:
        values = values * shard_levels(rng, dims, shards, -0.22, 0.18)
    return jnp.clip(values, -bound, bound).astype(kind)


def setup_inputs(seed: int = 0) -> dict:
    key_of = jax.random.split(jax.random.key(seed), 13)
    return {
        "hidden_in": bell_draw(key_of[0], (TOKENS, MODEL_WIDTH), 1.0, 6.0, ((0, 32),)),
        "cotangent": bell_draw(key_of[1], (TOKENS, MODEL_WIDTH), 1.0, 6.0, ((0, 32),)),
        "lengths": draw_lengths(jax.random.fold_in(key_of[12], 71), 0),
        "offsets": draw_offsets(jax.random.fold_in(key_of[12], 71), 0),
        "projection_weight": bell_draw(key_of[4], (MODEL_WIDTH, (QUERY_HEADS + 2 * KEY_VALUE_HEADS) * HEAD_SIZE), MODEL_WIDTH ** -0.5, 0.125, ((0, 8),)),
        "merge_weight": bell_draw(key_of[5], (QUERY_HEADS * HEAD_SIZE, MODEL_WIDTH), (QUERY_HEADS * HEAD_SIZE // 64) ** -0.5, 1.0, ((0, 8),)),
        "expand_weight": bell_draw(key_of[6], (MODEL_WIDTH, 2 * FF), MODEL_WIDTH ** -0.5, 0.125, ((0, 8),)),
        "down_weight": bell_draw(key_of[7], (FF, MODEL_WIDTH), FF ** -0.5, 0.078125, ((0, 8),)),
        "first_gain": jnp.clip(1.0 + 0.18 * jax.random.normal(key_of[8], (MODEL_WIDTH,), jnp.float32), 0.099609375, 1.8984375).astype(jnp.bfloat16),
        "second_gain": jnp.clip(1.0 + 0.18 * jax.random.normal(key_of[9], (MODEL_WIDTH,), jnp.float32), 0.099609375, 1.8984375).astype(jnp.bfloat16),
        "query_norm_scale": jnp.clip(1.0 + 0.18 * jax.random.normal(key_of[10], (HEAD_SIZE,), jnp.float32), 0.099609375, 1.8984375).astype(jnp.bfloat16),
        "key_gain": jnp.clip(1.0 + 0.18 * jax.random.normal(key_of[11], (HEAD_SIZE,), jnp.float32), 0.099609375, 1.8984375).astype(jnp.bfloat16),
    }


EPS = 1e-06
THETA = 1000000.0
NEGATIVE = -1e+30
HIGH = lax.Precision.HIGHEST

@jax.custom_vjp
def lower_half(v):
    return lax.optimization_barrier(v.astype(jnp.bfloat16)).astype(jnp.float32)

@jax.custom_vjp
def low_back(v):
    return v

def low_keep(v):
    return (lower_half(v), None)

def low_pass(kept, grad):
    return (grad,)

def back_keep(v):
    return (v, None)

def back_low(kept, grad):
    return (lower_half(grad),)
lower_half.defvjp(low_keep, low_pass)
low_back.defvjp(back_keep, back_low)

def layout(lengths, offsets):
    slots = jnp.arange(CAP, dtype=jnp.int32)
    inside = (slots[:, None] >= offsets[None, :]) & (slots[:, None] < offsets[None, :] + lengths[None, :])
    number = jnp.arange(NSEQ, dtype=jnp.int32) + 1
    segment = lax.optimization_barrier(jnp.sum(jnp.where(inside, number[None, :], 0), axis=1)) - 1
    position = lax.optimization_barrier(jnp.sum(jnp.where(inside, slots[:, None] - offsets[None, :], 0), axis=1))
    earlier = slots[None, :] <= slots[:, None]
    allowed = (segment[:, None] == segment[None, :]) & (segment[:, None] >= 0) & earlier
    allowed = allowed | (slots[None, :] == slots[:, None])
    expo = jnp.arange(HEAD_SIZE // 2, dtype=jnp.float32) * (2.0 / HEAD_SIZE)
    freq = jnp.power(THETA, -expo)
    angles = position.astype(jnp.float32)[:, None] * freq[None, :]
    return (allowed, jnp.cos(angles), jnp.sin(angles))

def apply_rotation(heads, cosine_table, sine_table):
    half = heads.shape[-1] // 2
    first = heads[..., :half]
    second = heads[..., half:]
    cosine_table = cosine_table[:, None, :]
    sine_table = sine_table[:, None, :]
    return jnp.concatenate([first * cosine_table - second * sine_table, second * cosine_table + first * sine_table], axis=-1)

def per_head_norm(heads, gain):
    return heads * lax.rsqrt(lax.optimization_barrier(jnp.mean(heads * heads, axis=-1, keepdims=True)) + EPS) * gain

def layer(tokens, allowed, cosine_table, sine_table, projection_weight, merge_weight, expand_weight, down_weight, first_gain, second_gain, query_norm_scale, key_gain):
    token_count = tokens.shape[0]
    head_group = QUERY_HEADS // KEY_VALUE_HEADS
    query_span = QUERY_HEADS * HEAD_SIZE
    key_span = KEY_VALUE_HEADS * HEAD_SIZE
    inverse_first = lax.rsqrt(lax.optimization_barrier(jnp.mean(tokens * tokens, axis=-1, keepdims=True)) + EPS)
    normed = lower_half(tokens * inverse_first * first_gain)
    combined_projection = low_back(jnp.dot(normed, projection_weight, precision=HIGH))
    query_rows = combined_projection[:, :query_span].reshape(token_count, QUERY_HEADS, HEAD_SIZE)
    key_rows = combined_projection[:, query_span:query_span + key_span].reshape(token_count, KEY_VALUE_HEADS, HEAD_SIZE)
    value_rows = lower_half(combined_projection[:, query_span + key_span:].reshape(token_count, KEY_VALUE_HEADS, HEAD_SIZE))
    query_rotated = lower_half(apply_rotation(per_head_norm(query_rows, query_norm_scale), cosine_table, sine_table)).reshape(token_count, KEY_VALUE_HEADS, head_group, HEAD_SIZE)
    key_rot = lower_half(apply_rotation(per_head_norm(key_rows, key_gain), cosine_table, sine_table))
    scale = 1.0 / math.sqrt(HEAD_SIZE)
    scores = low_back(jnp.einsum('qhgd,khd->hgqk', query_rotated, key_rot, precision=HIGH) * scale)
    masked = jnp.where(allowed, scores, NEGATIVE)
    top = lax.optimization_barrier(jnp.max(masked, axis=-1, keepdims=True))
    weights = jnp.where(allowed, jnp.exp(masked - top), 0.0)
    probs = weights / lax.optimization_barrier(jnp.sum(weights, axis=-1, keepdims=True))
    context = jnp.einsum('hgqk,khd->qhgd', lower_half(probs), value_rows, precision=HIGH)
    context = lower_half(low_back(context.reshape(token_count, query_span)))
    middle = tokens + low_back(jnp.dot(context, merge_weight, precision=HIGH))
    inverse_second = lax.rsqrt(lax.optimization_barrier(jnp.mean(middle * middle, axis=-1, keepdims=True)) + EPS)
    normed_second = lower_half(middle * inverse_second * second_gain)
    expanded = low_back(jnp.dot(normed_second, expand_weight, precision=HIGH))
    hidden = lower_half(jax.nn.silu(expanded[:, :FF]) * expanded[:, FF:])
    return middle + jnp.dot(hidden, down_weight, precision=HIGH)

def reference(hidden_in, cotangent, lengths, offsets, projection_weight, merge_weight, expand_weight, down_weight, first_gain, second_gain, query_norm_scale, key_gain):
    params = (projection_weight.astype(jnp.float32), merge_weight.astype(jnp.float32), expand_weight.astype(jnp.float32), down_weight.astype(jnp.float32), first_gain.astype(jnp.float32), second_gain.astype(jnp.float32), query_norm_scale.astype(jnp.float32), key_gain.astype(jnp.float32))
    devices = hidden_in.shape[0] // CAP
    rows_in = hidden_in.astype(jnp.float32).reshape(devices, CAP, MODEL_WIDTH)
    rows_back = cotangent.astype(jnp.float32).reshape(devices, CAP, MODEL_WIDTH)

    def one_device(totals, items):
        tokens, grad_rows, length_row, offset_row = items
        allowed, cosine_table, sine_table = layout(length_row, offset_row)

        def forward(tokens, *weights):
            return layer(tokens, allowed, cosine_table, sine_table, *weights)
        result, pull = jax.vjp(forward, tokens, *params)
        grads = pull(grad_rows)
        totals = tuple((total + grad for total, grad in zip(totals, grads[1:])))
        return (totals, (result.astype(jnp.bfloat16), grads[0].astype(jnp.bfloat16)))
    zeros = tuple((jnp.zeros_like(weight) for weight in params))
    totals, (results, input_rows) = lax.scan(one_device, zeros, (rows_in, rows_back, lengths, offsets))
    return (results.reshape(devices * CAP, MODEL_WIDTH), input_rows.reshape(devices * CAP, MODEL_WIDTH), totals[0], totals[1], totals[2], totals[3], totals[4], totals[5], totals[6], totals[7])
```

```python
import math

import jax
import jax.numpy as jnp
from jax import lax
from jax.sharding import PartitionSpec as P

QUERY_HEADS = 16
KEY_VALUE_HEADS = 8
HEAD_SIZE = 128
FF = 6144

EPS = 1e-06
THETA = 1000000.0
NEGATIVE = -1e30
LOW = jnp.bfloat16


def layout(lengths, offsets, slot_count):
    slots = jnp.arange(slot_count, dtype=jnp.int32)
    inside = (slots[:, None] >= offsets[None, :]) & (
        slots[:, None] < offsets[None, :] + lengths[None, :]
    )
    number = jnp.arange(lengths.shape[0], dtype=jnp.int32) + 1
    segment = jnp.sum(jnp.where(inside, number[None, :], 0), axis=1) - 1
    position = jnp.sum(jnp.where(inside, slots[:, None] - offsets[None, :], 0), axis=1)
    earlier = slots[None, :] <= slots[:, None]
    allowed = (segment[:, None] == segment[None, :]) & (segment[:, None] >= 0) & earlier
    allowed = allowed | (slots[None, :] == slots[:, None])
    expo = jnp.arange(HEAD_SIZE // 2, dtype=jnp.float32) * (2.0 / HEAD_SIZE)
    freq = jnp.power(THETA, -expo)
    angles = position.astype(jnp.float32)[:, None] * freq[None, :]
    return (allowed, jnp.cos(angles), jnp.sin(angles))


def apply_rotation(heads, cosine_table, sine_table):
    half = heads.shape[-1] // 2
    first = heads[..., :half]
    second = heads[..., half:]
    cosine_table = cosine_table[:, None, :]
    sine_table = sine_table[:, None, :]
    return jnp.concatenate(
        [first * cosine_table - second * sine_table, second * cosine_table + first * sine_table],
        axis=-1,
    )


def unrotate(grads, cosine_table, sine_table):
    half = grads.shape[-1] // 2
    first = grads[..., :half]
    second = grads[..., half:]
    cosine_table = cosine_table[:, None, :]
    sine_table = sine_table[:, None, :]
    return jnp.concatenate(
        [first * cosine_table + second * sine_table, second * cosine_table - first * sine_table],
        axis=-1,
    )


def norm_back(scaled, unit, inverse):
    return inverse * (scaled - unit * jnp.mean(scaled * unit, axis=-1, keepdims=True))


def times(left, right):
    return jnp.dot(left, right, preferred_element_type=jnp.float32)


def times_transposed(left, right):
    return lax.dot_general(
        left, right, (((1,), (1,)), ((), ())), preferred_element_type=jnp.float32
    )


def transposed_times(left, right):
    return lax.dot_general(
        left, right, (((0,), (0,)), ((), ())), preferred_element_type=jnp.float32
    )


def shards(
    shard_count,
    rep_count,
    hidden_in,
    cotangent,
    lengths,
    offsets,
    projection_weight,
    merge_weight,
    expand_weight,
    down_weight,
    first_gain,
    second_gain,
    query_norm_scale,
    key_gain,
):
    chips = shard_count // 2
    rank = lax.axis_index("shard")
    core = rank % 2
    chip = rank // 2
    slots, width = hidden_in.shape
    rows = width // shard_count
    group = QUERY_HEADS // KEY_VALUE_HEADS
    kv_heads = KEY_VALUE_HEADS // chips
    q_heads = QUERY_HEADS // chips
    q_cols = q_heads * HEAD_SIZE
    k_cols = kv_heads * HEAD_SIZE
    q_all = QUERY_HEADS * HEAD_SIZE
    k_all = KEY_VALUE_HEADS * HEAD_SIZE
    units = FF // chips
    scale = 1.0 / math.sqrt(HEAD_SIZE)

    def swap(x, mask):
        return lax.ppermute(x, "shard", [(i, i ^ mask) for i in range(shard_count)])

    def columns(w, start, size):
        return lax.dynamic_slice_in_dim(w, start, size, axis=1)

    def projection_part(t):
        return jnp.concatenate(
            [
                columns(projection_weight, t * q_cols, q_cols),
                columns(projection_weight, q_all + t * k_cols, k_cols),
                columns(projection_weight, q_all + k_all + t * k_cols, k_cols),
            ],
            axis=1,
        )

    def expand_part(t):
        return jnp.concatenate(
            [
                columns(expand_weight, t * units, units),
                columns(expand_weight, FF + t * units, units),
            ],
            axis=1,
        )

    def in_order(parts):
        stacked = jnp.zeros((chips,) + parts[0].shape, parts[0].dtype)
        for r, part in enumerate(parts):
            stacked = lax.dynamic_update_index_in_dim(stacked, part, chip ^ r, 0)
        return stacked

    def column_shard(part_of):
        parts = [part_of(chip)] + [swap(part_of(chip ^ r), 2 * r) for r in range(1, chips)]
        mine = in_order(parts).reshape(chips * rows, -1)
        return jnp.concatenate([mine, swap(mine, 1)], axis=0)

    def row_shard(w):
        other = swap(w, 1)
        return jnp.where(
            core == 0, jnp.concatenate([w, other], axis=0), jnp.concatenate([other, w], axis=0)
        )

    def relative(x):
        pieces = [x[:, j * rows : (j + 1) * rows] for j in range(shard_count)]
        even, odd = pieces[0::2], pieces[1::2]
        return jnp.where(
            core == 0, jnp.concatenate(even + odd, axis=1), jnp.concatenate(odd + even, axis=1)
        )

    def absolute(x):
        pieces = [x[:, j * rows : (j + 1) * rows] for j in range(shard_count)]
        mine, other = pieces[:chips], pieces[chips:]
        return jnp.where(
            core == 0,
            jnp.concatenate([p for pair in zip(mine, other) for p in pair], axis=1),
            jnp.concatenate([p for pair in zip(other, mine) for p in pair], axis=1),
        )

    def gather_blocks(x):
        return [x] + [swap(x, 2 * r) for r in range(1, chips)]

    def scatter_blocks(parts):
        total = parts[0]
        for r in range(1, chips):
            total = total + swap(parts[r].astype(LOW), 2 * r).astype(jnp.float32)
        return total

    heads_full = column_shard(projection_part)
    small = jnp.concatenate(
        [
            first_gain,
            second_gain,
            query_norm_scale,
            key_gain,
            lengths[0].astype(LOW),
            offsets[0].astype(LOW),
        ]
    )
    small_all = lax.all_gather(small, "shard", axis=0)
    head_rows = query_norm_scale.shape[0]
    entries = lengths.shape[1]
    ends = [0, rows, 2 * rows, 2 * rows + head_rows, 2 * rows + 2 * head_rows]
    first_scale, second_scale, query_scale, key_scale = (
        small_all[:, a:b].reshape(-1).astype(jnp.float32) for a, b in zip(ends[:-1], ends[1:])
    )
    placed = small_all[:, ends[-1] :].astype(jnp.int32)

    tokens = hidden_in.astype(jnp.float32)
    inverse_first = lax.rsqrt(jnp.mean(tokens * tokens, axis=1, keepdims=True) + EPS)
    unit_first = tokens * inverse_first
    normed = relative((unit_first * first_scale).astype(LOW))
    normed_blocks = gather_blocks(normed)
    merge_full = row_shard(merge_weight)

    saved = []
    merged_parts = []
    for r in range(chips):
        place = lax.dynamic_index_in_dim(placed, rank ^ (2 * r), 0, keepdims=False)
        allowed, cosine_table, sine_table = layout(place[:entries], place[entries:], slots)
        united = times(normed_blocks[r], heads_full)
        query_rows = united[:, :q_cols].reshape(slots, q_heads, HEAD_SIZE)
        key_rows = united[:, q_cols : q_cols + k_cols].reshape(slots, kv_heads, HEAD_SIZE)
        value_rows = united[:, q_cols + k_cols :].reshape(slots, kv_heads, HEAD_SIZE).astype(LOW)
        query_inverse = lax.rsqrt(jnp.mean(query_rows * query_rows, axis=-1, keepdims=True) + EPS)
        query_unit = query_rows * query_inverse
        key_inverse = lax.rsqrt(jnp.mean(key_rows * key_rows, axis=-1, keepdims=True) + EPS)
        key_unit = key_rows * key_inverse
        query_rot = (
            apply_rotation(query_unit * query_scale, cosine_table, sine_table)
            .astype(LOW)
            .reshape(slots, kv_heads, group, HEAD_SIZE)
        )
        key_rot = apply_rotation(key_unit * key_scale, cosine_table, sine_table).astype(LOW)
        scores = (
            jnp.einsum("qhgd,khd->hgqk", query_rot, key_rot, preferred_element_type=jnp.float32)
            * scale
        )
        masked = jnp.where(allowed, scores, NEGATIVE)
        top = jnp.max(masked, axis=-1, keepdims=True)
        weights = jnp.where(allowed, jnp.exp(masked - top), 0.0)
        probs = weights / jnp.sum(weights, axis=-1, keepdims=True)
        context = jnp.einsum(
            "hgqk,khd->qhgd", probs.astype(LOW), value_rows, preferred_element_type=jnp.float32
        )
        context = context.reshape(slots, q_cols).astype(LOW)
        merged_parts.append(times(context, merge_full))
        saved.append(
            (
                cosine_table,
                sine_table,
                query_unit,
                query_inverse,
                key_unit,
                key_inverse,
                query_rot,
                key_rot,
                value_rows,
                probs,
                context,
            )
        )
    middle = tokens + scatter_blocks(merged_parts)

    expand_full = column_shard(expand_part)
    down_full = row_shard(down_weight)
    cotangent_blocks = gather_blocks(cotangent)
    inverse_second = lax.rsqrt(jnp.mean(middle * middle, axis=1, keepdims=True) + EPS)
    unit_second = middle * inverse_second
    normed_second = relative((unit_second * second_scale).astype(LOW))
    second_blocks = gather_blocks(normed_second)
    output_parts = []
    second_parts = []
    hidden_blocks = []
    expand_blocks = []
    for r in range(chips):
        expanded = times(second_blocks[r], expand_full)
        gates = expanded[:, :units]
        ups = expanded[:, units:]
        sigmoid = jax.nn.sigmoid(gates)
        activated = gates * sigmoid
        hidden = (activated * ups).astype(LOW)
        output_parts.append(times(hidden, down_full))
        hidden_grad = times_transposed(cotangent_blocks[r], down_full)
        gate_grad = hidden_grad * ups * (sigmoid * (1.0 + gates * (1.0 - sigmoid)))
        up_grad = hidden_grad * activated
        expand_rows = jnp.concatenate([gate_grad, up_grad], axis=1).astype(LOW)
        second_parts.append(times_transposed(expand_rows, expand_full))
        hidden_blocks.append(hidden)
        expand_blocks.append(expand_rows)
    second_back = absolute(scatter_blocks(second_parts))
    output = (middle + scatter_blocks(output_parts)).astype(LOW)
    middle_grad = cotangent.astype(jnp.float32) + norm_back(
        second_back * second_scale, unit_second, inverse_second
    )

    attention_rows = middle_grad.astype(LOW)
    attention_blocks = gather_blocks(attention_rows)
    first_parts = []
    united_blocks = []
    query_term = jnp.zeros((HEAD_SIZE,), jnp.float32)
    key_term = jnp.zeros((HEAD_SIZE,), jnp.float32)
    for r in range(chips):
        (
            cosine_table,
            sine_table,
            query_unit,
            query_inverse,
            key_unit,
            key_inverse,
            query_rot,
            key_rot,
            value_rows,
            probs,
            context,
        ) = saved[r]
        context_grad = (
            times_transposed(attention_blocks[r], merge_full)
            .astype(LOW)
            .reshape(slots, kv_heads, group, HEAD_SIZE)
        )
        value_grad = jnp.einsum(
            "hgqk,qhgd->khd", probs.astype(LOW), context_grad, preferred_element_type=jnp.float32
        )
        probs_grad = jnp.einsum(
            "qhgd,khd->hgqk", context_grad, value_rows, preferred_element_type=jnp.float32
        )
        delta = jnp.sum(probs * probs_grad, axis=-1, keepdims=True)
        score_grad = (probs * (probs_grad - delta)).astype(LOW)
        query_rot_grad = (
            jnp.einsum(
                "hgqk,khd->qhgd", score_grad, key_rot, preferred_element_type=jnp.float32
            ).reshape(slots, q_heads, HEAD_SIZE)
            * scale
        )
        key_rot_grad = (
            jnp.einsum("hgqk,qhgd->khd", score_grad, query_rot, preferred_element_type=jnp.float32)
            * scale
        )
        query_normed_grad = unrotate(query_rot_grad, cosine_table, sine_table)
        key_normed_grad = unrotate(key_rot_grad, cosine_table, sine_table)
        query_term = query_term + jnp.sum(query_normed_grad * query_unit, axis=(0, 1))
        key_term = key_term + jnp.sum(key_normed_grad * key_unit, axis=(0, 1))
        query_back = norm_back(query_normed_grad * query_scale, query_unit, query_inverse)
        key_back = norm_back(key_normed_grad * key_scale, key_unit, key_inverse)
        united_rows = jnp.concatenate(
            [
                query_back.reshape(slots, q_cols),
                key_back.reshape(slots, k_cols),
                value_grad.reshape(slots, k_cols),
            ],
            axis=1,
        ).astype(LOW)
        first_parts.append(times_transposed(united_rows, heads_full))
        united_blocks.append(united_rows)
    first_back = absolute(scatter_blocks(first_parts))
    input_grad = (
        middle_grad + norm_back(first_back * first_scale, unit_first, inverse_first)
    ).astype(LOW)

    def core_sum(left_mine, left_other, right):
        other = swap(transposed_times(left_other, right).astype(LOW), 1)
        return (transposed_times(left_mine, right) + other.astype(jnp.float32)).astype(LOW)

    def by_columns(blocks, right):
        left = jnp.concatenate(blocks, axis=0)
        half = left.shape[1] // 2
        return core_sum(left[:, :half], left[:, half:], right)

    def by_rows(blocks, right):
        left = jnp.concatenate(blocks, axis=0)
        half = left.shape[1] // 2
        return core_sum(
            columns(left, core * half, half), columns(left, (1 - core) * half, half), right
        )

    def to_owner(total):
        stacked = total.reshape(chips, rows, -1)
        parts = []
        for r in range(chips):
            part = lax.dynamic_index_in_dim(stacked, chip ^ r, 0, keepdims=False)
            parts.append(part if r == 0 else swap(part, 2 * r))
        return in_order(parts)

    def side_by_side(stacked, *sizes):
        pieces = []
        start = 0
        for size in sizes:
            pieces += [stacked[j, :, start : start + size] for j in range(chips)]
            start += size
        return jnp.concatenate(pieces, axis=1).astype(jnp.float32)

    down_sum = lax.psum(by_rows(hidden_blocks, jnp.concatenate(cotangent_blocks)), "rep")
    expand_sum = lax.psum(by_columns(second_blocks, jnp.concatenate(expand_blocks)), "rep")
    merge_sum = lax.psum(
        by_rows([s[-1] for s in saved], jnp.concatenate(attention_blocks)), "rep"
    )
    heads_sum = lax.psum(by_columns(normed_blocks, jnp.concatenate(united_blocks)), "rep")
    down_grad = down_sum.astype(jnp.float32)
    merge_grad = merge_sum.astype(jnp.float32)
    expand_grad = side_by_side(to_owner(expand_sum), units, units)
    heads_grad = side_by_side(to_owner(heads_sum), q_cols, k_cols, k_cols)

    first_grad = jnp.sum(
        projection_weight.astype(jnp.float32) * heads_grad, axis=1
    ) / first_gain.astype(jnp.float32)
    second_grad = jnp.sum(
        expand_weight.astype(jnp.float32) * expand_grad, axis=1
    ) / second_gain.astype(jnp.float32)
    terms = lax.psum(jnp.concatenate([query_term, key_term]), ("rep", "shard"))
    query_grad = lax.dynamic_slice_in_dim(terms, rank * head_rows, head_rows)
    key_grad = lax.dynamic_slice_in_dim(terms, HEAD_SIZE + rank * head_rows, head_rows)
    return (
        output,
        input_grad,
        heads_grad,
        merge_grad,
        expand_grad,
        down_grad,
        first_grad,
        second_grad,
        query_grad,
        key_grad,
    )


def solution(mesh):
    tokens = P(("rep", "shard"), None)
    rows = P("shard", None)
    vector = P("shard")

    def step(*args):
        return shards(mesh.shape["shard"], mesh.shape["rep"], *args)

    return jax.shard_map(
        step,
        mesh=mesh,
        in_specs=(tokens,) * 4 + (rows,) * 4 + (vector,) * 4,
        out_specs=(tokens,) * 2 + (rows,) * 4 + (vector,) * 4,
        check_vma=False,
    )
```

```python
import functools
import math

import jax
import jax.numpy as jnp
from jax import lax
from jax.experimental import pallas as pl
from jax.experimental.pallas import tpu as pltpu
from jax.sharding import PartitionSpec as P

QUERY_HEADS = 16
KEY_VALUE_HEADS = 8
HEAD_SIZE = 128
FF = 6144

EPS = 1e-06
THETA = 1000000.0
NEGATIVE = -1e30
LOW = jnp.bfloat16
WIDE = jnp.float32
LIMIT = 58 * 1024 * 1024


def times(left, right):
    return jnp.dot(left, right, preferred_element_type=WIDE)


def times_transposed(left, right):
    return lax.dot_general(left, right, (((1,), (1,)), ((), ())), preferred_element_type=WIDE)


def transposed_times(left, right):
    return lax.dot_general(left, right, (((0,), (0,)), ((), ())), preferred_element_type=WIDE)


def call(kernel, name, scalars, grid, ins, outs, scratch=(), flops=0):
    moved = sum(a.size * a.dtype.itemsize for a, _, _ in ins)
    moved += sum(math.prod(s) * jnp.dtype(d).itemsize for s, d, _, _ in outs)
    return pl.pallas_call(
        kernel,
        name=name,
        out_shape=[jax.ShapeDtypeStruct(s, d) for s, d, _, _ in outs],
        grid_spec=pltpu.PrefetchScalarGridSpec(
            num_scalar_prefetch=1,
            grid=grid,
            in_specs=[pl.BlockSpec(b, m) for _, b, m in ins],
            out_specs=[pl.BlockSpec(b, m) for _, _, b, m in outs],
            scratch_shapes=list(scratch),
        ),
        compiler_params=pltpu.CompilerParams(vmem_limit_bytes=LIMIT),
        cost_estimate=pl.CostEstimate(flops=int(flops), bytes_accessed=int(moved), transcendentals=0),
    )(scalars, *[a for a, _, _ in ins])


def whole(a, *_):
    zeros = (0,) * a.ndim
    return (a, a.shape, lambda *_: zeros)


def whole_out(shape, dtype):
    zeros = (0,) * len(shape)
    return (shape, dtype, shape, lambda *_: zeros)


def by_row(a, tile):
    return (a, (tile, a.shape[1]), lambda i, *_: (i, 0))


def row_out(shape, dtype, tile):
    return (shape, dtype, (tile, shape[1]), lambda i, *_: (i, 0))


def relative_piece(j, core, chips):
    return ((j % 2) ^ core) * chips + j // 2


def lanes(start, size):
    return pl.ds(pl.multiple_of(start, 128), size)


def shards(
    shard_count,
    rep_count,
    hidden_in,
    cotangent,
    lengths,
    offsets,
    projection_weight,
    merge_weight,
    expand_weight,
    down_weight,
    first_gain,
    second_gain,
    query_norm_scale,
    key_gain,
):
    chips = shard_count // 2
    rank = lax.axis_index("shard")
    depth = lax.axis_index("rep")
    core = rank % 2
    chip = rank // 2
    slots, width = hidden_in.shape
    rows = width // shard_count
    half = width // 2
    group = QUERY_HEADS // KEY_VALUE_HEADS
    kv_heads = KEY_VALUE_HEADS // chips
    q_heads = QUERY_HEADS // chips
    q_cols = q_heads * HEAD_SIZE
    k_cols = kv_heads * HEAD_SIZE
    u_cols = q_cols + 2 * k_cols
    q_all = QUERY_HEADS * HEAD_SIZE
    k_all = KEY_VALUE_HEADS * HEAD_SIZE
    m_rows = merge_weight.shape[0]
    units = FF // chips
    h_units = units // 2
    share = rep_count % 2 == 0 and units % (rep_count * 128) == 0
    parts_count = rep_count if share else 2
    part_units = units // parts_count
    scale = 1.0 / math.sqrt(HEAD_SIZE)
    head_rows = query_norm_scale.shape[0]
    entries = lengths.shape[1]
    tile = slots // 4
    here = jnp.stack([core, chip]).astype(jnp.int32)

    def swap(x, mask):
        return lax.ppermute(x, "shard", [(i, i ^ mask) for i in range(shard_count)])

    def columns(w, start, size):
        return lax.dynamic_slice_in_dim(w, start, size, axis=1)

    def projection_part(t):
        return jnp.concatenate(
            [
                columns(projection_weight, t * q_cols, q_cols),
                columns(projection_weight, q_all + t * k_cols, k_cols),
                columns(projection_weight, q_all + k_all + t * k_cols, k_cols),
            ],
            axis=1,
        )

    def expand_part(t, g):
        return jnp.concatenate(
            [
                columns(expand_weight, t * units + g * part_units, part_units),
                columns(expand_weight, FF + t * units + g * part_units, part_units),
            ],
            axis=1,
        )

    def in_order(parts):
        stacked = jnp.zeros((chips,) + parts[0].shape, parts[0].dtype)
        for r, part in enumerate(parts):
            stacked = lax.dynamic_update_index_in_dim(stacked, part, chip ^ r, 0)
        return stacked

    def to_chips(part_of):
        return [part_of(chip)] + [swap(part_of(chip ^ r), 2 * r) for r in range(1, chips)]

    def gather_blocks(x):
        return [x] + [swap(x, 2 * r) for r in range(1, chips)]

    def send_back(parts):
        return [parts[0]] + [swap(parts[r], 2 * r) for r in range(1, chips)]

    def gather_pair(low, high):
        blocks = [(low, high)]
        for r in range(1, 3 if chips == 4 else chips):
            blocks.append((swap(low, 2 * r), swap(high, 2 * r)))
        return blocks

    def relay_pair(blocks):
        if chips == 4:
            low, high = line(blocks[1][0], blocks[2][1])
            blocks.append((swap(low, 4), swap(high, 2)))
        return blocks

    tokens_seen = []

    def line(*xs):
        if not tokens_seen:
            return xs if len(xs) > 1 else xs[0]
        out = lax.optimization_barrier((*xs, tokens_seen[-1]))[:-1]
        return out if len(out) > 1 else out[0]

    def mark(x):
        tokens_seen.append(x)

    if share:
        quarter_parts = to_chips(lambda t: expand_part(t, depth))
    else:
        quarter_parts = [
            to_chips(lambda t, g=g: expand_part(t, g)) for g in range(parts_count)
        ]
    heads_mine = to_chips(projection_part)
    vectors = [
        first_gain,
        second_gain,
        query_norm_scale,
        key_gain,
        lengths[0].astype(LOW),
        offsets[0].astype(LOW),
    ]
    ends = [0]
    for v in vectors:
        ends.append(ends[-1] + v.shape[0])
    padded = -(-ends[-1] // 128) * 128
    small = jnp.concatenate(vectors + [jnp.zeros((padded - ends[-1],), LOW)])
    small_all = lax.all_gather(small.reshape(1, padded), "shard", axis=0, tiled=True)
    first_scale, second_scale, query_scale, key_scale, all_lengths, all_offsets = (
        small_all[:, a:b].astype(WIDE) for a, b in zip(ends[:-1], ends[1:])
    )
    first_scale, second_scale, query_scale, key_scale = (
        s.reshape(1, -1) for s in (first_scale, second_scale, query_scale, key_scale)
    )

    def split_relative(s, y, mine_ref, other_ref):
        for p in range(chips):
            even = y[:, 2 * p * rows : (2 * p + 1) * rows]
            odd = y[:, (2 * p + 1) * rows : (2 * p + 2) * rows]
            mine_ref[:, p * rows : (p + 1) * rows] = jnp.where(s[0] == 0, even, odd)
            other_ref[:, p * rows : (p + 1) * rows] = jnp.where(s[0] == 0, odd, even)

    def first_kernel(s, x_ref, gain_ref, mine_ref, other_ref):
        x = x_ref[...].astype(WIDE)
        inverse = lax.rsqrt(jnp.mean(x * x, axis=1, keepdims=True) + EPS)
        split_relative(s, (x * inverse * gain_ref[...]).astype(LOW), mine_ref, other_ref)

    normed = call(
        first_kernel,
        "first_norm",
        here,
        (slots // tile,),
        [by_row(hidden_in, tile), whole(first_scale)],
        [row_out((slots, half), LOW, tile)] * 2,
    )
    mark(normed[0])
    normed_blocks = gather_pair(*normed)
    merge_other = swap(line(merge_weight), 1)
    down_other_rows = swap(line(down_weight), 1)

    slot = jnp.arange(slots, dtype=jnp.int32)
    expo = jnp.arange(HEAD_SIZE // 2, dtype=WIDE) * (2.0 / HEAD_SIZE)
    freq = jnp.power(THETA, -expo)
    owners = jnp.stack([rank ^ (2 * r) for r in range(chips)])
    begin = all_offsets[owners].astype(jnp.int32)
    extent = all_lengths[owners].astype(jnp.int32)
    inside = (slot[None, :, None] >= begin[:, None, :]) & (
        slot[None, :, None] < (begin + extent)[:, None, :]
    )
    position = jnp.sum(jnp.where(inside, slot[None, :, None] - begin[:, None, :], 0), axis=2)
    angles = position.astype(WIDE)[:, :, None] * freq[None, None, :]
    cosine, sine = jnp.cos(angles), jnp.sin(angles)
    turn = jnp.concatenate([cosine, cosine, -sine, sine], axis=2)
    placed = jnp.concatenate(
        [jnp.broadcast_to(here[None], (chips, 2)), begin, begin + extent], axis=1
    )

    if share:
        quarter = in_order(line(*quarter_parts))
        mark(quarter)
        expand_mine = lax.all_gather(quarter, "rep", axis=0, tiled=False)
    else:
        expand_mine = jnp.stack([in_order(p) for p in quarter_parts])
    heads_mine = list(line(*heads_mine))
    heads_other = [swap(w, 1) for w in heads_mine]
    heads_pieces = heads_mine + heads_other

    def allowed_pairs(s):
        row = lax.broadcasted_iota(jnp.int32, (slots, 1), 0)
        col = lax.broadcasted_iota(jnp.int32, (1, slots), 1)
        row_seg = jnp.zeros((slots, 1), jnp.int32)
        col_seg = jnp.zeros((1, slots), jnp.int32)
        for k in range(entries):
            lo, hi = s[2 + k], s[2 + entries + k]
            row_seg = row_seg + jnp.where((row >= lo) & (row < hi), k + 1, 0)
            col_seg = col_seg + jnp.where((col >= lo) & (col < hi), k + 1, 0)
        same = (row_seg == col_seg) & (row_seg > 0) & (col <= row)
        return same | (col == row)

    def rotate(v, turn_ref):
        return v * turn_ref[:, :HEAD_SIZE] + pltpu.roll(v, HEAD_SIZE // 2, 1) * turn_ref[:, HEAD_SIZE:]

    def unrotate(g, turn_ref):
        return g * turn_ref[:, :HEAD_SIZE] - pltpu.roll(g, HEAD_SIZE // 2, 1) * turn_ref[:, HEAD_SIZE:]

    def unit_of(v):
        inverse = lax.rsqrt(jnp.mean(v * v, axis=1, keepdims=True) + EPS)
        return v * inverse, inverse

    def attend_kernel(s, xm_ref, xo_ref, turn_ref, qs_ref, ks_ref, mine_ref, other_ref, *rest):
        w_refs, (part_ref, united_ref, probs_ref, ctx_ref) = rest[: 2 * chips], rest[2 * chips :]
        total = None
        for r in range(chips):
            for side, x_ref in enumerate((xm_ref, xo_ref)):
                at = (s[1] ^ r) * rows
                term = times(x_ref[:, lanes(at, rows)], w_refs[side * chips + r][...])
                total = term if total is None else total + term
        united_ref[...] = total
        allowed = allowed_pairs(s)
        for g in range(kv_heads):
            key = united_ref[:, q_cols + g * HEAD_SIZE : q_cols + (g + 1) * HEAD_SIZE]
            key_rot = rotate(unit_of(key)[0] * ks_ref[...], turn_ref).astype(LOW)
            at = q_cols + k_cols + g * HEAD_SIZE
            value = united_ref[:, at : at + HEAD_SIZE].astype(LOW)
            for h in range(g * group, (g + 1) * group):
                span = slice(h * HEAD_SIZE, (h + 1) * HEAD_SIZE)
                query = united_ref[:, span]
                query_rot = rotate(unit_of(query)[0] * qs_ref[...], turn_ref).astype(LOW)
                scores = times_transposed(query_rot, key_rot) * scale
                masked = jnp.where(allowed, scores, NEGATIVE)
                top = jnp.max(masked, axis=1, keepdims=True)
                weights = jnp.where(allowed, jnp.exp(masked - top), 0.0)
                probs = (weights / jnp.sum(weights, axis=1, keepdims=True)).astype(LOW)
                probs_ref[h] = probs
                ctx_ref[:, span] = times(probs, value).astype(LOW)
        part = times(ctx_ref[:, lanes(s[0] * m_rows, m_rows)], mine_ref[...])
        part = part + times(ctx_ref[:, lanes((1 - s[0]) * m_rows, m_rows)], other_ref[...])
        part_ref[...] = part.astype(LOW)

    merged, united_saved, probs_saved, contexts = [], [], [], []

    def attend(r):
        block = line(*normed_blocks[r])
        part, united, probs, context = call(
            attend_kernel,
            "attend",
            placed[r],
            (1,),
            [
                whole(a)
                for a in [*block, turn[r], query_scale, key_scale, merge_weight, merge_other]
                + heads_pieces
            ],
            [
                whole_out((slots, width), LOW),
                whole_out((slots, u_cols), WIDE),
                whole_out((q_heads, slots, slots), LOW),
                whole_out((slots, q_cols), LOW),
            ],
            flops=2 * slots * width * (u_cols + q_cols),
        )
        mark(part)
        merged.append(part if r == 0 else swap(part, 2 * r))
        united_saved.append(united)
        probs_saved.append(probs)
        contexts.append(context)

    attend(0)
    relay_pair(normed_blocks)
    for r in range(1, chips - 1):
        attend(r)
    cotangent_pair = line(*normed_blocks[-1], cotangent[:, :half], cotangent[:, half:])
    normed_blocks[-1] = cotangent_pair[:2]
    cotangent_blocks = gather_pair(*cotangent_pair[2:])
    attend(chips - 1)
    relay_pair(cotangent_blocks)

    def second_kernel(s, x_ref, gain_ref, *rest):
        part_refs, (middle_ref, mine_ref, other_ref) = rest[:chips], rest[chips:]
        x = x_ref[...].astype(WIDE)
        for ref in part_refs:
            x = x + ref[...].astype(WIDE)
        middle_ref[...] = x
        inverse = lax.rsqrt(jnp.mean(x * x, axis=1, keepdims=True) + EPS)
        split_relative(s, (x * inverse * gain_ref[...]).astype(LOW), mine_ref, other_ref)

    middle, *normed_second = call(
        second_kernel,
        "second_norm",
        here,
        (slots // tile,),
        [by_row(hidden_in, tile), whole(second_scale)] + [by_row(p, tile) for p in line(*merged)],
        [row_out((slots, width), WIDE, tile)] + [row_out((slots, half), LOW, tile)] * 2,
    )
    mark(middle)
    second_blocks = gather_pair(*normed_second)
    expand_mine = line(expand_mine)
    expand_other = swap(expand_mine, 1)
    down_both = jnp.stack([down_weight, line(down_other_rows)])
    mark(down_both)
    relay_pair(second_blocks)

    def feed_kernel(s, xm_ref, xo_ref, mine_ref, other_ref, hid_ref, slope_ref):
        w_mine = mine_ref[0].reshape(half, 2 * part_units)
        w_other = other_ref[0].reshape(half, 2 * part_units)
        both = times(xm_ref[...], w_mine) + times(xo_ref[...], w_other)
        gates, ups = both[:, :part_units], both[:, part_units:]
        sigmoid = 1.0 / (1.0 + jnp.exp(-gates))
        activated = gates * sigmoid
        hid_ref[...] = (activated * ups).astype(LOW)
        slope_ref[:, :part_units] = (ups * (sigmoid * (1.0 + gates * (1.0 - sigmoid)))).astype(LOW)
        slope_ref[:, part_units:] = activated.astype(LOW)

    hidden_blocks, slopes = [], []

    def feed(r):
        block = (1, chips, rows, 2 * part_units)
        hid, slope = call(
            feed_kernel,
            "feed",
            here,
            (parts_count,),
            [whole(a) for a in line(*second_blocks[r])]
            + [
                (expand_mine, block, lambda i, s: (i, 0, 0, 0)),
                (expand_other, block, lambda i, s: (i, 0, 0, 0)),
            ],
            [
                ((slots, units), LOW, (slots, part_units), lambda i, s: (0, i)),
                ((slots, 2 * units), LOW, (slots, 2 * part_units), lambda i, s: (0, i)),
            ],
            flops=4 * slots * width * units,
        )
        mark(hid)
        hidden_blocks.append(hid)
        slopes.append(slope)

    step_parts = parts_count // 2

    def feed_back_kernel(s, cl_ref, ch_ref, slope_ref, mine_ref, other_ref, down_ref, back_ref, grad_ref, back_sum):
        step = pl.program_id(0)

        @pl.when(step == 0)
        def _():
            back_sum[...] = jnp.zeros_like(back_sum)

        hidden_grads = times_transposed(cl_ref[...], down_ref[0, :, :half]) + times_transposed(
            ch_ref[...], down_ref[0, :, half:]
        )
        for q in range(step_parts):
            w_mine = mine_ref[q].reshape(half, 2 * part_units)
            w_other = other_ref[q].reshape(half, 2 * part_units)
            hidden_grad = hidden_grads[:, q * part_units : (q + 1) * part_units]
            at = 2 * q * part_units
            for side in range(2):
                span = slice(at + side * part_units, at + (side + 1) * part_units)
                grad_ref[:, span] = (hidden_grad * slope_ref[:, span].astype(WIDE)).astype(LOW)
            grads = grad_ref[:, at : at + 2 * part_units]
            back_sum[:, :half] += times_transposed(grads, w_mine)
            back_sum[:, half:] += times_transposed(grads, w_other)

        @pl.when(step == 1)
        def _():
            back_ref[...] = back_sum[...].astype(LOW)

    second_back, grad_blocks = [], []

    def feed_back(r):
        block = (step_parts, chips, rows, 2 * part_units)
        back, grad = call(
            feed_back_kernel,
            "feed_back",
            here,
            (2,),
            [whole(a) for a in line(*cotangent_blocks[r])]
            + [
                (slopes[r], (slots, units), lambda i, s: (0, i ^ s[0])),
                (expand_mine, block, lambda i, s: (i ^ s[0], 0, 0, 0)),
                (expand_other, block, lambda i, s: (i ^ s[0], 0, 0, 0)),
                (down_both, (1, h_units, width), lambda i, s: (i, 0, 0)),
            ],
            [
                whole_out((slots, width), LOW),
                ((slots, 2 * units), LOW, (slots, units), lambda i, s: (0, i ^ s[0])),
            ],
            scratch=[pltpu.VMEM((slots, width), WIDE)],
            flops=6 * slots * width * units,
        )
        mark(grad)
        second_back.append(back if r == 0 else swap(back, 2 * r))
        grad_blocks.append(grad)

    def grad_kernel(count, splits, has_other, s, *refs):
        lefts, rights = refs[:chips], refs[chips : chips * (1 + count // splits)]
        others = refs[len(refs) - 2 * count : len(refs) - count] if has_other else None
        outs = refs[-count:]
        size = outs[0].shape[1]
        left = jnp.concatenate([ref[...].T for ref in lefts], axis=1)
        for k in range(count):
            total = None
            for r in range(chips):
                right = rights[(k // splits) * chips + r]
                at = (k % splits) * size
                term = times(left[:, r * slots : (r + 1) * slots], right[:, at : at + size])
                total = term if total is None else total + term
            if has_other:
                total = total + others[k][...].astype(WIDE)
            outs[k][...] = total.astype(LOW)

    def grad_half(name, lefts, rights, start, length, splits, others=None):
        step = min(256, length)
        n = rights[0][0].shape[1]
        count = len(rights) * splits
        lefts = line(*lefts)
        ins = [(a, (slots, step), lambda i, s: (0, start(s) // step + i)) for a in lefts]
        ins += [whole(a) for blocks in rights for a in blocks]
        if others is not None:
            ins += [by_row(a, step) for a in others]
        out = call(
            functools.partial(grad_kernel, count, splits, others is not None),
            name,
            here,
            (length // step,),
            ins,
            [row_out((length, n // splits), LOW, step) for _ in range(count)],
            flops=2 * slots * chips * length * n * len(rights),
        )
        mark(out[0])
        return out

    def zero(_):
        return 0

    def halves(blocks):
        return [[b[0] for b in blocks], [b[1] for b in blocks]]

    def from_core(parts):
        return [swap(a, 1) for a in parts]

    in_middle = (depth == 1) | (depth == 2)

    class Sum:
        def __init__(self, x):
            self.x = x
            if rep_count == 4:
                self.came = lax.ppermute(x, "rep", [(0, 1), (3, 2)])

        def across(self):
            if rep_count == 4:
                came, x = line(self.came, self.x)
                self.x = x + came
                mark(self.x)
                self.came = lax.ppermute(self.x, "rep", [(1, 2), (2, 1)])

        def outward(self):
            if rep_count == 4:
                came, x = line(self.came, self.x)
                self.x = x + came
                mark(self.x)
                self.came = lax.ppermute(self.x, "rep", [(1, 0), (2, 3)])

        def result(self):
            if rep_count != 4:
                return lax.psum(self.x, "rep")
            x, came = line(self.x, self.came)
            return jnp.where(in_middle, x, came)

    for r in range(chips):
        feed(r)
    cotangent_halves = halves(cotangent_blocks)
    down_came = from_core(
        grad_half("down_other", hidden_blocks, cotangent_halves, lambda s: (1 - s[0]) * h_units, h_units, 1)
    )
    feed_back(0)
    down_parts = grad_half(
        "down_mine", hidden_blocks, cotangent_halves, lambda s: s[0] * h_units, h_units, 1, down_came
    )
    down_sums = [Sum(a) for a in down_parts]
    for r in range(1, chips):
        feed_back(r)
    second_halves = halves(second_blocks)
    expand_came = from_core(
        grad_half("expand_other", second_halves[1], [grad_blocks], zero, half, parts_count)
    )
    down_sums[0].across()

    def pieces_sum(s, refs, j):
        at = relative_piece(j, s[0], chips) * rows
        total = refs[0][:, lanes(at, rows)].astype(WIDE)
        for ref in refs[1:]:
            total = total + ref[:, lanes(at, rows)].astype(WIDE)
        return total

    def norm_back(x, grad, gain):
        unit, inverse = unit_of(x)
        scaled = grad * gain
        return inverse * (scaled - unit * jnp.mean(scaled * unit, axis=1, keepdims=True))

    def middle_kernel(s, c_ref, middle_ref, gain_ref, *rest):
        part_refs, (grad_ref, low_ref, high_ref) = rest[:chips], rest[chips:]
        back = jnp.concatenate([pieces_sum(s, part_refs, j) for j in range(shard_count)], axis=1)
        grad = c_ref[...].astype(WIDE) + norm_back(middle_ref[...], back, gain_ref[...])
        grad_ref[...] = grad
        low_ref[...] = grad[:, :half].astype(LOW)
        high_ref[...] = grad[:, half:].astype(LOW)

    middle_grad, *attention_rows = call(
        middle_kernel,
        "middle_back",
        here,
        (slots // tile,),
        [by_row(cotangent, tile), by_row(middle, tile), whole(second_scale)]
        + [by_row(p, tile) for p in line(*second_back)],
        [row_out((slots, width), WIDE, tile)] + [row_out((slots, half), LOW, tile)] * 2,
    )
    mark(middle_grad)
    attention_blocks = gather_pair(*attention_rows)
    expand_parts = grad_half(
        "expand_mine", second_halves[0], [grad_blocks], zero, half, parts_count, expand_came
    )
    expand_sums = [Sum(a) for a in expand_parts]
    down_sums[1].across()

    def attend_back_kernel(s, al_ref, ah_ref, united_ref, probs_ref, turn_ref, qs_ref, ks_ref, mine_ref, other_ref, *rest):
        w_refs, (grad_ref, part_ref, term_ref, ctx_ref) = rest[: 2 * chips], rest[2 * chips :]
        for place, m_ref in ((s[0], mine_ref), (1 - s[0], other_ref)):
            back = times_transposed(al_ref[...], m_ref[:, :half]) + times_transposed(ah_ref[...], m_ref[:, half:])
            ctx_ref[:, lanes(place * m_rows, m_rows)] = back.astype(LOW)
        query_term = jnp.zeros((1, HEAD_SIZE), WIDE)
        key_term = jnp.zeros((1, HEAD_SIZE), WIDE)
        for g in range(kv_heads):
            key_span = slice(q_cols + g * HEAD_SIZE, q_cols + (g + 1) * HEAD_SIZE)
            value_span = slice(q_cols + k_cols + g * HEAD_SIZE, q_cols + k_cols + (g + 1) * HEAD_SIZE)
            key_unit, key_inverse = unit_of(united_ref[:, key_span])
            key_rot = rotate(key_unit * ks_ref[...], turn_ref).astype(LOW)
            value = united_ref[:, value_span].astype(LOW)
            value_grad = jnp.zeros((slots, HEAD_SIZE), WIDE)
            key_grad = jnp.zeros((slots, HEAD_SIZE), WIDE)
            for h in range(g * group, (g + 1) * group):
                span = slice(h * HEAD_SIZE, (h + 1) * HEAD_SIZE)
                query_unit, query_inverse = unit_of(united_ref[:, span])
                query_rot = rotate(query_unit * qs_ref[...], turn_ref).astype(LOW)
                probs = probs_ref[h]
                context_grad = ctx_ref[:, span]
                value_grad = value_grad + transposed_times(probs, context_grad)
                probs_grad = times_transposed(context_grad, value)
                wide = probs.astype(WIDE)
                delta = jnp.sum(wide * probs_grad, axis=1, keepdims=True)
                score_grad = (wide * (probs_grad - delta)).astype(LOW)
                key_grad = key_grad + transposed_times(score_grad, query_rot)
                normed_grad = unrotate(times(score_grad, key_rot) * scale, turn_ref)
                query_term = query_term + jnp.sum(normed_grad * query_unit, axis=0, keepdims=True)
                scaled = normed_grad * qs_ref[...]
                back = query_inverse * (
                    scaled - query_unit * jnp.mean(scaled * query_unit, axis=1, keepdims=True)
                )
                grad_ref[:, span] = back.astype(LOW)
            normed_grad = unrotate(key_grad * scale, turn_ref)
            key_term = key_term + jnp.sum(normed_grad * key_unit, axis=0, keepdims=True)
            scaled = normed_grad * ks_ref[...]
            back = key_inverse * (scaled - key_unit * jnp.mean(scaled * key_unit, axis=1, keepdims=True))
            grad_ref[:, key_span] = back.astype(LOW)
            grad_ref[:, value_span] = value_grad.astype(LOW)
        term_ref[...] = jnp.concatenate([query_term, key_term, jnp.zeros((6, HEAD_SIZE), WIDE)], axis=0)
        for r in range(chips):
            for side in range(2):
                at = side * half + (s[1] ^ r) * rows
                part = times_transposed(grad_ref[...], w_refs[side * chips + r][...])
                part_ref[:, lanes(at, rows)] = part.astype(LOW)

    united_blocks, first_back, terms = [], [], []

    def attend_back(r):
        grad, part, term = call(
            attend_back_kernel,
            "attend_back",
            placed[r],
            (1,),
            [
                whole(a)
                for a in [
                    *line(*attention_blocks[r]),
                    united_saved[r],
                    probs_saved[r],
                    turn[r],
                    query_scale,
                    key_scale,
                    merge_weight,
                    merge_other,
                ]
                + heads_pieces
            ],
            [
                whole_out((slots, u_cols), LOW),
                whole_out((slots, width), LOW),
                whole_out((8, HEAD_SIZE), WIDE),
            ],
            scratch=[pltpu.VMEM((slots, q_cols), LOW)],
            flops=2 * slots * width * (u_cols + q_cols),
        )
        mark(part)
        united_blocks.append(grad)
        first_back.append(part if r == 0 else swap(part, 2 * r))
        terms.append(term)

    attend_back(0)
    down_sums[0].outward()
    relay_pair(attention_blocks)
    for r in range(1, chips - 1):
        attend_back(r)
    expand_sums[0].across()
    down_sums[1].outward()
    attend_back(chips - 1)

    normed_halves = halves(normed_blocks)
    attention_halves = halves(attention_blocks)
    heads_came = from_core(grad_half("heads_other", normed_halves[1], [united_blocks], zero, half, 1))
    merge_came = from_core(
        grad_half("merge_other", contexts, attention_halves, lambda s: (1 - s[0]) * m_rows, m_rows, 1)
    )
    expand_sums[1].across()
    heads_part = grad_half("heads_mine", normed_halves[0], [united_blocks], zero, half, 1, heads_came)[0]

    def owner_pieces(total):
        stacked = total.reshape(chips, rows, -1)
        return [lax.dynamic_index_in_dim(stacked, chip ^ r, 0, keepdims=False) for r in range(chips)]

    def send_pieces(pieces):
        return [pieces[0]] + [swap(pieces[r], 2 * r) for r in range(1, chips)]

    heads_sent = send_pieces(owner_pieces(heads_part))
    merge_parts = grad_half(
        "merge_mine", contexts, attention_halves, lambda s: s[0] * m_rows, m_rows, 1, merge_came
    )

    def input_kernel(s, x_ref, grad_ref, gain_ref, *rest):
        back = jnp.concatenate([pieces_sum(s, rest[:chips], j) for j in range(shard_count)], axis=1)
        x = x_ref[...].astype(WIDE)
        rest[chips][...] = (grad_ref[...] + norm_back(x, back, gain_ref[...])).astype(LOW)

    (input_grad,) = call(
        input_kernel,
        "input_back",
        here,
        (slots // tile,),
        [by_row(hidden_in, tile), by_row(middle_grad, tile), whole(first_scale)]
        + [by_row(p, tile) for p in line(*first_back)],
        [row_out((slots, width), LOW, tile)],
    )
    mark(input_grad)
    expand_sums[0].outward()
    heads_owned = in_order(line(*heads_sent))
    mark(heads_owned)
    heads_sums = [Sum(heads_owned[: chips // 2]), Sum(heads_owned[chips // 2 :])]
    merge_sums = [Sum(a) for a in merge_parts]
    expand_sums[2 % parts_count].across() if parts_count > 2 else None

    def feed_out_kernel(s, hid_ref, down_ref, out_ref):
        mine = hid_ref[:, lanes(s[0] * h_units, h_units)]
        other = hid_ref[:, lanes((1 - s[0]) * h_units, h_units)]
        out_ref[...] = (times(mine, down_ref[0]) + times(other, down_ref[1])).astype(LOW)

    output_parts = []
    for r in range(chips):
        (part,) = call(
            feed_out_kernel,
            "feed_out",
            here,
            (2,),
            [
                whole(line(hidden_blocks[r])),
                (down_both, (2, h_units, half), lambda i, s: (0, 0, i)),
            ],
            [((slots, width), LOW, (slots, half), lambda i, s: (0, i))],
            flops=2 * slots * width * units,
        )
        mark(part)
        output_parts.append(part if r == 0 else swap(part, 2 * r))

    expand_sums[1].outward()
    if parts_count > 3:
        expand_sums[3].across()
        expand_sums[2].outward()

    def output_kernel(s, middle_ref, *rest):
        total = middle_ref[...]
        for ref in rest[:chips]:
            total = total + ref[...].astype(WIDE)
        rest[chips][...] = total.astype(LOW)

    (output,) = call(
        output_kernel,
        "output",
        here,
        (slots // tile,),
        [by_row(middle, tile)] + [by_row(p, tile) for p in line(*output_parts)],
        [row_out((slots, width), LOW, tile)],
    )
    mark(output)

    term = sum(terms[1:], terms[0])
    bit = 1
    while bit < shard_count:
        term = term + swap(term, bit)
        bit *= 2
    bit = 1
    while bit < rep_count:
        term = term + lax.ppermute(term, "rep", [(i, i ^ bit) for i in range(rep_count)])
        bit *= 2
    query_grad = lax.dynamic_slice_in_dim(term[0], rank * head_rows, head_rows)
    key_grad = lax.dynamic_slice_in_dim(term[1], rank * head_rows, head_rows)

    expand_owned = []

    def own_expand(k):
        pieces = send_pieces(owner_pieces(expand_sums[k].result()))
        expand_owned.append(pieces)

    heads_sums[0].across()
    if parts_count > 3:
        expand_sums[3].outward()
    own_expand(0)
    heads_sums[1].across()
    heads_sums[0].outward()
    own_expand(1)
    merge_sums[0].across()
    heads_sums[1].outward()
    if parts_count > 2:
        own_expand(2)
    merge_sums[1].across()
    merge_sums[0].outward()
    if parts_count > 3:
        own_expand(3)
    merge_sums[1].outward()
    for k in range(4, parts_count):
        own_expand(k)

    down_grad = jnp.concatenate([x.result() for x in down_sums], axis=1).astype(WIDE)
    expand_owned = [in_order(p) for p in expand_owned]
    expand_grad = jnp.concatenate(
        [a[j, :, :part_units] for j in range(chips) for a in expand_owned]
        + [a[j, :, part_units:] for j in range(chips) for a in expand_owned],
        axis=1,
    ).astype(WIDE)
    heads_total = jnp.concatenate([x.result() for x in heads_sums], axis=0)
    heads_grad = jnp.concatenate(
        [heads_total[j, :, :q_cols] for j in range(chips)]
        + [heads_total[j, :, q_cols : q_cols + k_cols] for j in range(chips)]
        + [heads_total[j, :, q_cols + k_cols :] for j in range(chips)],
        axis=1,
    ).astype(WIDE)
    merge_grad = jnp.concatenate([x.result() for x in merge_sums], axis=1).astype(WIDE)

    first_grad = jnp.sum(projection_weight.astype(WIDE) * heads_grad, axis=1) / first_gain.astype(WIDE)
    second_grad = jnp.sum(expand_weight.astype(WIDE) * expand_grad, axis=1) / second_gain.astype(WIDE)
    return (
        output,
        input_grad,
        heads_grad,
        merge_grad,
        expand_grad,
        down_grad,
        first_grad,
        second_grad,
        query_grad,
        key_grad,
    )


def solution(mesh):
    tokens = P(("rep", "shard"), None)
    rows = P("shard", None)
    vector = P("shard")

    def step(*args):
        return shards(mesh.shape["shard"], mesh.shape["rep"], *args)

    return jax.shard_map(
        step,
        mesh=mesh,
        in_specs=(tokens,) * 4 + (rows,) * 4 + (vector,) * 4,
        out_specs=(tokens,) * 2 + (rows,) * 4 + (vector,) * 4,
        check_vma=False,
    )
```
